32 devices in a mesh: row: 8 (over z, core), col: 4 (over y, x).
Axes of the slice: x: 2, y: 2, z: 4, core: 2. Of those that a mesh axis runs over, the one named last changes fastest.
Arguments:
- density: bfloat16 [8192, 8192], P('row', 'col'), may hold values from -6 to 6
- listed: int32 [64, 64], P('row', 'col'), may hold values 0 or 1
- three_centre: bfloat16 [128, 512, 512], P(('row', 'col')), may hold values from -0.25 to 0.25
Outputs:
- exchange_diag: float32 [8192, 512], P('row', 'col')
- exchange_density: bfloat16 [8192, 8192], P('row', 'col')
The draws below stay inside these ranges and needn't reach their ends.
All inputs are finite; a program needn't handle non-finite values. No bound on the sum of `listed` on one device may be relied on, other than what follows from the above.
Results may differ from the reference program's by a relative error of at most 0.0058.
Values may be sent and summed in bfloat16 or wider, within the bound.
A program may use at most 64 MiB of HBM per device.

```python
import jax
import jax.numpy as jnp
from jax import lax

TILE = 128
NT = 64
NB = 8192
W = 512
AUX_DEV = 4
TR = 8
NGS = 2
AUX = 128
AUX_GROUP = 8
N_COL = 4


def plant(result, key, least, high):
    place = [jax.random.randint(jax.random.fold_in(key, axis), (), 0, length) for axis, length in enumerate(result.shape)]
    widest = result.shape.index(max(result.shape))
    next_to = place[:widest] + [(place[widest] + 1) % result.shape[widest]] + place[widest + 1:]
    return result.at[tuple(place)].set(least).at[tuple(next_to)].set(high)


def block_scale(stream_key, shape, pieces, smallest, high):
    factor_of, own = 1.0, jax.random.fold_in(stream_key, 6)
    for position, shards_of in pieces:
        heights = jnp.exp(jax.random.uniform(jax.random.fold_in(own, position), (shards_of,), jnp.float32, smallest / len(pieces), high / len(pieces)))
        factor_of = factor_of * jnp.repeat(heights, shape[position] // shards_of).reshape([-1 if axis == position else 1 for axis in range(len(shape))])
    return factor_of


def normal_values(key, dims, scale, most, cuts=(), held_as=jnp.bfloat16):
    array = scale * jax.random.normal(key, dims, jnp.float32)
    if cuts:
        array = array * block_scale(key, dims, cuts, -0.22, 0.18)
    return jnp.clip(array, -most, most).astype(held_as)


def setup_inputs(seed: int = 0) -> dict:
    key_list = jax.random.split(jax.random.key(seed), 4)
    density = normal_values(key_list[0], (NB, NB), 1.0, 6.0, ((0, 8), (1, 4)))
    listed = plant((jax.random.randint(key_list[1], (NT, NT), 0, 2) < 1).astype(jnp.int32), jax.random.fold_in(key_list[1], 1), 0, 1)
    three_centre = normal_values(key_list[2], (AUX, W, W), W ** -0.5, 0.25, ((0, 32),))
    return dict(density=density, listed=listed, three_centre=three_centre)


def reference(density, listed, three_centre):
    masked = (density.reshape(NT, TILE, NT, TILE) * listed[:, None, :, None].astype(jnp.bfloat16)).reshape(NB, NB)
    group_total = NT // 4
    aux_index = jnp.arange(AUX, dtype=jnp.int32)
    device = aux_index // AUX_DEV
    row_pos = device // N_COL
    col_pos = device % N_COL
    aux_slot = aux_index % AUX_DEV
    support = ((row_pos * TR) // 4 + (col_pos * AUX_DEV + aux_slot) % NGS).astype(jnp.int32)

    def accumulate(blocks, item):
        aux_block, group_id = item
        start = (group_id * W).astype(jnp.int32)
        density_sub = lax.dynamic_slice(masked, (start, start), (W, W))
        half_product = jnp.dot(aux_block, density_sub, preferred_element_type=jnp.float32).astype(jnp.bfloat16)
        contribution = jnp.dot(half_product, aux_block.T, preferred_element_type=jnp.float32)
        return blocks.at[group_id].add(contribution), None

    blocks, _ = lax.scan(accumulate, jnp.zeros((group_total, W, W), jnp.float32), (three_centre, support))
    blocks = blocks * (AUX_GROUP ** -0.5)
    exchange_diag = blocks.reshape(NB, W)
    rounded = blocks.astype(jnp.bfloat16)

    def apply_group(group_id):
        dens_rows = lax.dynamic_slice_in_dim(masked, (group_id * W).astype(jnp.int32), W, 0)
        product = jnp.dot(rounded[group_id], dens_rows, preferred_element_type=jnp.float32) * (W ** -0.5)
        return product.astype(jnp.bfloat16)

    exchange_density = lax.map(apply_group, jnp.arange(group_total, dtype=jnp.int32)).reshape(NB, NB)
    return exchange_diag, exchange_density
```

```python
import functools

import jax
import jax.numpy as jnp
from jax import lax
from jax.experimental import pallas as pl
from jax.experimental.pallas import tpu as pltpu
from jax.sharding import PartitionSpec as P

TILE = 128
W = 512
SUP = W // TILE
HALF = W // 2
MESH = pl.DeviceIdType.MESH


def from_root(value, axis, root):
    mine = lax.axis_index(axis) == root
    return lax.psum(jnp.where(mine, value, jnp.zeros_like(value)), axis)


def partner_2(block, axis, stride):
    count = lax.axis_size(axis)
    route = []
    for low in range(count):
        high = low | 1 << stride
        if high != low and high < count:
            route += [(low, high), (high, low)]
    return lax.ppermute(block, axis, route)


def halve_rows(values, row_index, levels, sender):
    for bit_level in reversed(range(levels)):
        middle = values.shape[0] // 2
        lower_half = row_index // 2**bit_level % 2 == 0
        kept_rows = jnp.where(lower_half, values[:middle], values[middle:])
        sent_rows = jnp.where(lower_half, values[middle:], values[:middle])
        values = kept_rows + sender(sent_rows, bit_level)
    return values


def per_device(density, listed, three_centre):
    tile_rows = listed.shape[0]
    tile_cols = listed.shape[1]
    quad_tiles = max(tile_rows, 4)
    groups_dev = quad_tiles // 4
    aux_count = three_centre.shape[0]
    col_count = lax.axis_size("col")
    row_index = lax.axis_index("row")
    col_index = lax.axis_index("col")
    masked = (
        density.reshape(tile_rows, TILE, tile_cols, TILE)
        * listed[:, None, :, None].astype(jnp.bfloat16)
    ).reshape(tile_rows * TILE, tile_cols * TILE)
    quad_start = row_index * tile_rows // quad_tiles * quad_tiles
    col_offset = quad_start % tile_cols * TILE
    portion = lax.dynamic_slice_in_dim(masked, col_offset, quad_tiles * TILE, 1)
    diagonal = from_root(portion, "col", quad_start // tile_cols)
    joined = jnp.concatenate([diagonal, masked], axis=1)
    levels = (quad_tiles // tile_rows).bit_length() - 1
    for bit_level in range(levels):
        partner = partner_2(joined, "row", bit_level)
        lower_half = row_index // 2**bit_level % 2 == 0
        joined = jnp.where(
            lower_half,
            jnp.concatenate([joined, partner], axis=0),
            jnp.concatenate([partner, joined], axis=0),
        )
    quad_block = joined[:, : quad_tiles * TILE]
    quad_density = joined[:, quad_tiles * TILE :]
    group_ids = jnp.arange(groups_dev, dtype=jnp.int32)
    exchange_quad = jnp.zeros((groups_dev, W, W), jnp.float32)
    for aux_slot in range(aux_count):
        group_slot = (col_index * aux_count + aux_slot) % groups_dev
        density_sub = lax.dynamic_slice(quad_block, (group_slot * W, group_slot * W), (W, W))
        aux_block = three_centre[aux_slot]
        half_product = jnp.dot(aux_block, density_sub, preferred_element_type=jnp.float32).astype(
            jnp.bfloat16
        )
        contribution = lax.dot_general(
            half_product, aux_block, (((1,), (1,)), ((), ())), preferred_element_type=jnp.float32
        )
        exchange_quad = exchange_quad + jnp.where(
            (group_ids == group_slot)[:, None, None], contribution[None], 0.0
        )
    aux_group = aux_count * col_count * 4 // tile_rows
    exchange_quad = (exchange_quad * aux_group ** (-0.5)).reshape(quad_tiles * TILE, W)
    column_share = lax.psum_scatter(exchange_quad, "col", scatter_dimension=1, tiled=True)
    exchange_diag = halve_rows(
        column_share,
        row_index,
        levels,
        lambda sent_rows, bit_level: partner_2(sent_rows, "row", bit_level),
    )
    fock_rounded = lax.all_gather(exchange_diag.astype(jnp.bfloat16), "col", axis=1, tiled=True)
    rows_here = tile_rows * TILE
    segment_rows = min(rows_here, W)
    segment_count = rows_here // segment_rows
    within_quad = (row_index * tile_rows - quad_start) * TILE
    products = []
    for segment in range(segment_count):
        group_position = (within_quad + segment * segment_rows) // W
        dens_rows = lax.dynamic_slice_in_dim(quad_density, group_position * W, W, 0)
        fock_part = fock_rounded[segment * segment_rows : (segment + 1) * segment_rows]
        products.append(
            jnp.dot(fock_part, dens_rows, preferred_element_type=jnp.float32) * W ** (-0.5)
        )
    exchange_density = jnp.concatenate(products, axis=0).astype(jnp.bfloat16)
    return (exchange_diag, exchange_density)


def mask_tile(tile, flag):
    return (tile.astype(jnp.float32) * flag.astype(jnp.float32)).astype(jnp.bfloat16)


def exchange_kernel(
    scale, listed, density, three_centre, diag_out, fock_out,
    raw, block, coef, partial, send_1, recv_1, send_2, recv_2, fock,
    raw_sem, coef_sem, bc_send, bc_recv, rs1_send, rs1_recv, rs2_send, rs2_recv,
    ag1_send, ag1_recv, ag2_send, ag2_recv,
):
    tile_rows, tile_cols = listed.shape
    groups = tile_rows // SUP
    aux_count = three_centre.shape[0]
    row = lax.axis_index("row")
    me = lax.axis_index("col")
    x, y = me % 2, me // 2
    xn, yn = me + 1 - 2 * x, me + 2 - 4 * y
    first_tile = row * tile_rows
    owner = first_tile // tile_cols
    tile_off = first_tile % tile_cols
    ox, oy = owner % 2, owner // 2
    rx, ry = (x + ox) % 2, (y + oy) % 2
    even = (rx + ry + 1) % 2
    is_owner = rx + ry == 0
    hop_to = (xn * even + yn * (1 - even), yn * even + xn * (1 - even))
    last_of = (rx + 2 * (1 - ry) == 0, ry + 2 * (1 - rx) == 0)

    def remote(src, dst, send_sem, recv_sem, target):
        return pltpu.make_async_remote_copy(
            src_ref=src, dst_ref=dst, send_sem=send_sem, recv_sem=recv_sem,
            device_id=(row, target), device_id_type=MESH,
        )

    def raw_copy(g):
        columns = pl.ds(pl.multiple_of((tile_off + g * SUP) * TILE, TILE), W)
        return pltpu.make_async_copy(
            density.at[pl.ds(g * W, W), columns], raw.at[g], raw_sem.at[g]
        )

    def coef_copy(q):
        return pltpu.make_async_copy(three_centre.at[q], coef.at[q], coef_sem.at[q])

    def piece(g, i):
        part = block.at[g, pl.ds(i * TILE, TILE)]
        return remote(part, part, bc_send.at[g, i], bc_recv.at[g, i], hop_to[i // (SUP // 2)])

    @pl.when(is_owner)
    def _():
        for g in range(groups):
            raw_copy(g).start()

    barrier = pltpu.get_barrier_semaphore()
    for neighbour in (xn, yn):
        pl.semaphore_signal(barrier, inc=1, device_id=(row, neighbour), device_id_type=MESH)
    for q in range(aux_count):
        coef_copy(q).start()
    pl.semaphore_wait(barrier, 2)

    order = [s + h * (SUP // 2) for s in range(SUP // 2) for h in range(2)]

    @pl.when(is_owner)
    def _():
        for g in range(groups):
            raw_copy(g).wait()
            for i in order:
                for j in range(SUP):
                    rows, cols = pl.ds(i * TILE, TILE), pl.ds(j * TILE, TILE)
                    flag = listed[g * SUP + i, tile_off + g * SUP + j]
                    block[g, rows, cols] = mask_tile(raw[g, rows, cols], flag)
                piece(g, i).start()

    @pl.when(jnp.logical_not(is_owner))
    def _():
        for g in range(groups):
            for i in order:
                @pl.when(jnp.logical_not(last_of[i // (SUP // 2)]))
                def _():
                    piece(g, i).wait_recv()
                    piece(g, i).start()

    for q in range(aux_count):
        coef_copy(q).wait()

    near = (xn, yn)

    def stage_1(g, h):
        return remote(send_1.at[g, h], recv_1.at[g, h], rs1_send.at[g, h], rs1_recv.at[g, h], near[h])

    def stage_2(g, h):
        return remote(
            send_2.at[g, h], recv_2.at[g, h], rs2_send.at[g, h], rs2_recv.at[g, h], near[1 - h]
        )

    def columns_of(dev):
        return pl.ds(pl.multiple_of(dev * TILE, TILE), TILE)

    def gather_1(g, axis):
        part = fock.at[pl.ds(g * W, W), columns_of(me)]
        return remote(part, part, ag1_send.at[g, axis], ag1_recv.at[g, axis], near[axis])

    def gather_2(g, axis):
        part = fock.at[pl.ds(g * W + axis * HALF, HALF), columns_of(near[1 - axis])]
        return remote(part, part, ag2_send.at[g, axis], ag2_recv.at[g, axis], near[axis])

    def rows_of(h):
        return pl.ds(h * HALF, HALF)

    far = me + (xn - me) + (yn - me)
    for g in range(groups):
        for h in range(2):
            @pl.when(last_of[h])
            def _():
                for s in range(SUP // 2):
                    piece(g, s + h * (SUP // 2)).wait_recv()
        for n, q in enumerate(range(g, aux_count, groups)):
            half = jnp.dot(coef[q], block[g], preferred_element_type=jnp.float32).astype(jnp.bfloat16)
            term = lax.dot_general(
                half, coef[q], (((1,), (1,)), ((), ())), preferred_element_type=jnp.float32
            )
            if n == 0:
                partial[g] = term
            else:
                partial[g] += term
        for h in range(2):
            send_1[g, h, 0] = partial[g, rows_of(h), columns_of(near[h])].astype(jnp.bfloat16)
            send_1[g, h, 1] = partial[g, rows_of(h), columns_of(far)].astype(jnp.bfloat16)
            stage_1(g, h).start()
    for g in range(groups):
        for h in range(2):
            stage_1(g, h).wait_recv()
            send_2[g, h] = (
                partial[g, rows_of(h), columns_of(near[1 - h])] + recv_1[g, h, 1].astype(jnp.float32)
            ).astype(jnp.bfloat16)
            stage_2(g, h).start()
    for g in range(groups):
        for h in range(2):
            stage_2(g, h).wait_recv()
            total = (
                partial[g, rows_of(h), columns_of(me)]
                + recv_1[g, h, 0].astype(jnp.float32)
                + recv_2[g, h].astype(jnp.float32)
            ) * scale
            rows = pl.ds(g * W + h * HALF, HALF)
            diag_out[rows] = total
            fock[rows, columns_of(me)] = total.astype(jnp.bfloat16)
        for axis in range(2):
            gather_1(g, axis).start()
    for g in range(groups):
        for axis in range(2):
            gather_1(g, 1 - axis).wait_recv()
            gather_2(g, axis).start()
    for g in range(groups):
        for axis in range(2):
            gather_2(g, axis).wait_recv()
    fock_out[...] = fock[...]
    for g in range(groups):
        for i in range(SUP):
            @pl.when(jnp.logical_not(last_of[i // (SUP // 2)]))
            def _():
                piece(g, i).wait_send()
        for h in range(2):
            stage_1(g, h).wait_send()
            stage_2(g, h).wait_send()
            gather_1(g, h).wait_send()
            gather_2(g, h).wait_send()


def apply_kernel(listed, fock, density, result, masked):
    g, n = pl.program_id(0), pl.program_id(1)
    tiles = density.shape[1] // TILE
    for i in range(SUP):
        for j in range(tiles):
            rows, cols = slice(i * TILE, (i + 1) * TILE), slice(j * TILE, (j + 1) * TILE)
            masked[rows, cols] = mask_tile(density[rows, cols], listed[g * SUP + i, n * tiles + j])
    product = jnp.dot(fock[...], masked[...], preferred_element_type=jnp.float32)
    result[...] = (product * W ** (-0.5)).astype(jnp.bfloat16)


def per_device_whole(density, listed, three_centre):
    rows, cols = density.shape
    groups = rows // W
    aux_count = three_centre.shape[0]
    aux_group = aux_count * lax.axis_size("col") // groups
    bf16, dma = jnp.bfloat16, pltpu.SemaphoreType.DMA
    vmem = pl.BlockSpec(memory_space=pltpu.VMEM)
    anywhere = pl.BlockSpec(memory_space=pl.ANY)
    diag, fock = pl.pallas_call(
        functools.partial(exchange_kernel, aux_group ** (-0.5)),
        out_shape=(
            jax.ShapeDtypeStruct((rows, TILE), jnp.float32),
            jax.ShapeDtypeStruct((rows, W), bf16),
        ),
        in_specs=[pl.BlockSpec(memory_space=pltpu.SMEM), anywhere, anywhere],
        out_specs=(vmem, vmem),
        scratch_shapes=[
            pltpu.VMEM((groups, W, W), bf16),
            pltpu.VMEM((groups, W, W), bf16),
            pltpu.VMEM((aux_count, W, W), bf16),
            pltpu.VMEM((groups, W, W), jnp.float32),
            pltpu.VMEM((groups, 2, 2, HALF, TILE), bf16),
            pltpu.VMEM((groups, 2, 2, HALF, TILE), bf16),
            pltpu.VMEM((groups, 2, HALF, TILE), bf16),
            pltpu.VMEM((groups, 2, HALF, TILE), bf16),
            pltpu.VMEM((rows, W), bf16),
            dma((groups,)),
            dma((aux_count,)),
            dma((groups, SUP)),
            dma((groups, SUP)),
        ]
        + [dma((groups, 2)) for _ in range(8)],
        compiler_params=pltpu.CompilerParams(collective_id=0, has_side_effects=True),
    )(listed, density, three_centre)
    wide = min(cols, 1024)
    result = pl.pallas_call(
        apply_kernel,
        out_shape=jax.ShapeDtypeStruct((rows, cols), bf16),
        grid=(groups, cols // wide),
        in_specs=[
            pl.BlockSpec(memory_space=pltpu.SMEM),
            pl.BlockSpec((W, W), lambda g, n: (g, 0)),
            pl.BlockSpec((W, wide), lambda g, n: (g, n)),
        ],
        out_specs=pl.BlockSpec((W, wide), lambda g, n: (g, n)),
        scratch_shapes=[pltpu.VMEM((W, wide), bf16)],
    )(listed, fock, density)
    return diag, result


def takes_whole(mesh, density, listed, three_centre):
    row_count, col_count = mesh.shape["row"], mesh.shape["col"]
    rows = density.shape[0] // row_count
    cols = density.shape[1] // col_count
    aux_count = three_centre.shape[0] // (row_count * col_count)
    if rows % W or cols % rows or col_count != 4 or col_count * TILE != W:
        return False
    return aux_count % (rows // W) == 0


def solution(mesh):
    placed = (P("row", "col"), P("row", "col"), P(("row", "col"), None, None))

    def mapped(body):
        return jax.shard_map(
            body,
            mesh=mesh,
            in_specs=placed,
            out_specs=(P("row", "col"), P("row", "col")),
            check_vma=False,
        )

    def run(density, listed, three_centre):
        whole = takes_whole(mesh, density, listed, three_centre)
        return mapped(per_device_whole if whole else per_device)(density, listed, three_centre)

    return run
```

```python
import functools

import jax
import jax.numpy as jnp
from jax import lax
from jax.experimental import pallas as pl
from jax.experimental.pallas import tpu as pltpu
from jax.sharding import PartitionSpec as P

TILE = 128
W = 512
SUP = W // TILE
UNIT = W // 2
PART = UNIT // 2
PIECE = TILE // 2
MESH = pl.DeviceIdType.MESH


def from_root(value, axis, root):
    mine = lax.axis_index(axis) == root
    return lax.psum(jnp.where(mine, value, jnp.zeros_like(value)), axis)


def partner_2(block, axis, stride):
    count = lax.axis_size(axis)
    route = []
    for low in range(count):
        high = low | 1 << stride
        if high != low and high < count:
            route += [(low, high), (high, low)]
    return lax.ppermute(block, axis, route)


def halve_rows(values, row_index, levels, sender):
    for bit_level in reversed(range(levels)):
        middle = values.shape[0] // 2
        lower_half = row_index // 2**bit_level % 2 == 0
        kept_rows = jnp.where(lower_half, values[:middle], values[middle:])
        sent_rows = jnp.where(lower_half, values[middle:], values[:middle])
        values = kept_rows + sender(sent_rows, bit_level)
    return values


def per_device(density, listed, three_centre):
    tile_rows = listed.shape[0]
    tile_cols = listed.shape[1]
    quad_tiles = max(tile_rows, 4)
    groups_dev = quad_tiles // 4
    aux_count = three_centre.shape[0]
    col_count = lax.axis_size("col")
    row_index = lax.axis_index("row")
    col_index = lax.axis_index("col")
    masked = (
        density.reshape(tile_rows, TILE, tile_cols, TILE)
        * listed[:, None, :, None].astype(jnp.bfloat16)
    ).reshape(tile_rows * TILE, tile_cols * TILE)
    quad_start = row_index * tile_rows // quad_tiles * quad_tiles
    col_offset = quad_start % tile_cols * TILE
    portion = lax.dynamic_slice_in_dim(masked, col_offset, quad_tiles * TILE, 1)
    diagonal = from_root(portion, "col", quad_start // tile_cols)
    joined = jnp.concatenate([diagonal, masked], axis=1)
    levels = (quad_tiles // tile_rows).bit_length() - 1
    for bit_level in range(levels):
        partner = partner_2(joined, "row", bit_level)
        lower_half = row_index // 2**bit_level % 2 == 0
        joined = jnp.where(
            lower_half,
            jnp.concatenate([joined, partner], axis=0),
            jnp.concatenate([partner, joined], axis=0),
        )
    quad_block = joined[:, : quad_tiles * TILE]
    quad_density = joined[:, quad_tiles * TILE :]
    group_ids = jnp.arange(groups_dev, dtype=jnp.int32)
    exchange_quad = jnp.zeros((groups_dev, W, W), jnp.float32)
    for aux_slot in range(aux_count):
        group_slot = (col_index * aux_count + aux_slot) % groups_dev
        density_sub = lax.dynamic_slice(quad_block, (group_slot * W, group_slot * W), (W, W))
        aux_block = three_centre[aux_slot]
        half_product = jnp.dot(aux_block, density_sub, preferred_element_type=jnp.float32).astype(
            jnp.bfloat16
        )
        contribution = lax.dot_general(
            half_product, aux_block, (((1,), (1,)), ((), ())), preferred_element_type=jnp.float32
        )
        exchange_quad = exchange_quad + jnp.where(
            (group_ids == group_slot)[:, None, None], contribution[None], 0.0
        )
    aux_group = aux_count * col_count * 4 // tile_rows
    exchange_quad = (exchange_quad * aux_group ** (-0.5)).reshape(quad_tiles * TILE, W)
    column_share = lax.psum_scatter(exchange_quad, "col", scatter_dimension=1, tiled=True)
    exchange_diag = halve_rows(
        column_share,
        row_index,
        levels,
        lambda sent_rows, bit_level: partner_2(sent_rows, "row", bit_level),
    )
    fock_rounded = lax.all_gather(exchange_diag.astype(jnp.bfloat16), "col", axis=1, tiled=True)
    rows_here = tile_rows * TILE
    segment_rows = min(rows_here, W)
    segment_count = rows_here // segment_rows
    within_quad = (row_index * tile_rows - quad_start) * TILE
    products = []
    for segment in range(segment_count):
        group_position = (within_quad + segment * segment_rows) // W
        dens_rows = lax.dynamic_slice_in_dim(quad_density, group_position * W, W, 0)
        fock_part = fock_rounded[segment * segment_rows : (segment + 1) * segment_rows]
        products.append(
            jnp.dot(fock_part, dens_rows, preferred_element_type=jnp.float32) * W ** (-0.5)
        )
    exchange_density = jnp.concatenate(products, axis=0).astype(jnp.bfloat16)
    return (exchange_diag, exchange_density)


def mask_tile(tile, flag):
    return tile * jnp.full(tile.shape, flag.astype(jnp.float32)).astype(jnp.bfloat16)


def exchange_kernel(
    scale, listed, density, three_centre, diag_out, fock_out,
    raw, block, coef, half, partial, send_1, recv_1, send_2, recv_2, diag, fock,
    raw_sem, coef_sem, diag_sem, fock_sem, bc_send, bc_recv, rs1_send, rs1_recv,
    rs2_send, rs2_recv, ag1_send, ag1_recv, ag2_send, ag2_recv,
):
    tile_rows, tile_cols = listed.shape
    groups = tile_rows // SUP
    units = groups * (W // UNIT)
    aux_count = three_centre.shape[0]
    row = lax.axis_index("row")
    me = lax.axis_index("col")
    x, y = me % 2, me // 2
    xn, yn = me + 1 - 2 * x, me + 2 - 4 * y
    far = xn + yn - me
    near = (xn, yn)
    first_tile = row * tile_rows
    owner = first_tile // tile_cols
    tile_off = first_tile % tile_cols
    ox, oy = owner % 2, owner // 2
    rx, ry = (x + ox) % 2, (y + oy) % 2
    even = (rx + ry + 1) % 2
    is_owner = rx + ry == 0
    hop_to = (xn * even + yn * (1 - even), yn * even + xn * (1 - even))
    last_of = (rx + 2 * (1 - ry) == 0, ry + 2 * (1 - rx) == 0)
    relays_of = (
        (rx + ry) * (rx + 1 - ry) > 0,
        (rx + ry) * (ry + 1 - rx) > 0,
    )

    def remote(src, dst, send_sem, recv_sem, target):
        return pltpu.make_async_remote_copy(
            src_ref=src, dst_ref=dst, send_sem=send_sem, recv_sem=recv_sem,
            device_id=(row, target), device_id_type=MESH,
        )

    def raw_copy(g):
        columns = pl.ds(pl.multiple_of((tile_off + g * SUP) * TILE, TILE), W)
        return pltpu.make_async_copy(
            density.at[pl.ds(g * W, W), columns], raw.at[g], raw_sem.at[g]
        )

    def coef_copy(q):
        return pltpu.make_async_copy(three_centre.at[q], coef.at[q], coef_sem.at[q])

    per_path = W // PIECE // 2

    def piece(g, i):
        part = block.at[g, pl.ds(i * PIECE, PIECE)]
        return remote(part, part, bc_send.at[g, i], bc_recv.at[g, i], hop_to[i // per_path])

    @pl.when(is_owner)
    def _():
        for g in range(groups):
            raw_copy(g).start()

    barrier = pltpu.get_barrier_semaphore()
    for neighbour in near:
        pl.semaphore_signal(barrier, inc=1, device_id=(row, neighbour), device_id_type=MESH)
    for q in range(aux_count):
        coef_copy(q).start()
    pl.semaphore_wait(barrier, 2)

    order = [s + h * per_path for s in range(per_path) for h in range(2)]

    @pl.when(is_owner)
    def _():
        for g in range(groups):
            raw_copy(g).wait()
            for i in order:
                rows = pl.ds(i * PIECE, PIECE)
                for j in range(SUP):
                    cols = pl.ds(j * TILE, TILE)
                    flag = listed[g * SUP + i * PIECE // TILE, tile_off + g * SUP + j]
                    block[g, rows, cols] = mask_tile(raw[g, rows, cols], flag)
                piece(g, i).start()

    def relay(g, pieces):
        if g == groups:
            return
        for i in pieces:
            @pl.when(relays_of[i // per_path])
            def _():
                piece(g, i).wait_recv()
                piece(g, i).start()

    def stage_1(u, h):
        return remote(send_1.at[u, h], recv_1.at[u, h], rs1_send.at[u, h], rs1_recv.at[u, h], near[h])

    def stage_2(u, h):
        return remote(
            send_2.at[u, h], recv_2.at[u, h], rs2_send.at[u, h], rs2_recv.at[u, h], near[1 - h]
        )

    def columns_of(dev):
        return pl.ds(pl.multiple_of(dev * TILE, TILE), TILE)

    def rows_of(u, h):
        return pl.ds(u * UNIT + h * PART, PART)

    def gather_1(u, axis):
        part = fock.at[pl.ds(u * UNIT, UNIT), columns_of(me)]
        return remote(part, part, ag1_send.at[u, axis], ag1_recv.at[u, axis], near[axis])

    def gather_2(u, axis):
        part = fock.at[rows_of(u, axis), columns_of(near[1 - axis])]
        return remote(part, part, ag2_send.at[u, axis], ag2_recv.at[u, axis], near[axis])

    def diag_copy(u):
        rows = pl.ds(u * UNIT, UNIT)
        return pltpu.make_async_copy(diag.at[rows], diag_out.at[rows], diag_sem.at[u])

    def fock_copy(u):
        rows = pl.ds(u * UNIT, UNIT)
        return pltpu.make_async_copy(fock.at[rows], fock_out.at[rows], fock_sem.at[u])

    relay(0, order)
    for q in range(aux_count):
        coef_copy(q).wait()
    quarter = len(order) // 4
    for g in range(groups):
        members = list(range(g, aux_count, groups))
        relay(g + 1, order[:quarter])
        for h in range(2):
            @pl.when(last_of[h])
            def _():
                for s in range(per_path):
                    piece(g, s + h * per_path).wait_recv()
        for n, q in enumerate(members):
            half[n] = jnp.dot(coef[q], block[g], preferred_element_type=jnp.float32).astype(jnp.bfloat16)
            if n < 2:
                relay(g + 1, order[(n + 1) * quarter : (n + 2) * quarter])
        for v in range(W // UNIT):
            u = g * (W // UNIT) + v
            rows = pl.ds(v * UNIT, UNIT)
            for n, q in enumerate(members):
                term = lax.dot_general(
                    half[n, rows], coef[q], (((1,), (1,)), ((), ())),
                    preferred_element_type=jnp.float32,
                )
                if n == 0:
                    partial[pl.ds(u * UNIT, UNIT)] = term
                else:
                    partial[pl.ds(u * UNIT, UNIT)] += term
            for h in range(2):
                send_1[u, h, 0] = partial[rows_of(u, h), columns_of(near[h])].astype(jnp.bfloat16)
                send_1[u, h, 1] = partial[rows_of(u, h), columns_of(far)].astype(jnp.bfloat16)
                stage_1(u, h).start()
        relay(g + 1, order[(min(len(members), 2) + 1) * quarter :])

    for step in range(units + 3):
        if step < units:
            u = step
            for h in range(2):
                stage_1(u, h).wait_recv()
                send_2[u, h] = (
                    partial[rows_of(u, h), columns_of(near[1 - h])]
                    + recv_1[u, h, 1].astype(jnp.float32)
                ).astype(jnp.bfloat16)
                stage_2(u, h).start()
        if 1 <= step <= units:
            u = step - 1
            for h in range(2):
                stage_2(u, h).wait_recv()
                total = (
                    partial[rows_of(u, h), columns_of(me)]
                    + recv_1[u, h, 0].astype(jnp.float32)
                    + recv_2[u, h].astype(jnp.float32)
                ) * scale
                diag[rows_of(u, h)] = total
                fock[rows_of(u, h), columns_of(me)] = total.astype(jnp.bfloat16)
            for axis in range(2):
                gather_1(u, axis).start()
            diag_copy(u).start()
        if 2 <= step <= units + 1:
            u = step - 2
            for axis in range(2):
                gather_1(u, 1 - axis).wait_recv()
                gather_2(u, axis).start()
        if 3 <= step:
            u = step - 3
            for axis in range(2):
                gather_2(u, axis).wait_recv()
            fock_copy(u).start()
    for g in range(groups):
        for i in order:
            @pl.when(jnp.logical_not(last_of[i // per_path]))
            def _():
                piece(g, i).wait_send()
    for u in range(units):
        for h in range(2):
            stage_1(u, h).wait_send()
            stage_2(u, h).wait_send()
            gather_1(u, h).wait_send()
            gather_2(u, h).wait_send()
        diag_copy(u).wait()
        fock_copy(u).wait()


def apply_kernel(listed, fock, density, diag, result, diag_out, masked):
    g, n = pl.program_id(0), pl.program_id(1)
    tiles = density.shape[1] // TILE
    for i in range(SUP):
        for j in range(tiles):
            rows, cols = slice(i * TILE, (i + 1) * TILE), slice(j * TILE, (j + 1) * TILE)
            masked[rows, cols] = mask_tile(density[rows, cols], listed[g * SUP + i, n * tiles + j])
    product = jnp.dot(fock[...], masked[...], preferred_element_type=jnp.float32)
    result[...] = (product * W ** (-0.5)).astype(jnp.bfloat16)

    @pl.when(n == 0)
    def _():
        diag_out[...] = diag[...]


def per_device_whole(density, listed, three_centre):
    rows, cols = density.shape
    groups = rows // W
    units = rows // UNIT
    aux_count = three_centre.shape[0]
    aux_group = aux_count * lax.axis_size("col") // groups
    bf16, dma = jnp.bfloat16, pltpu.SemaphoreType.DMA
    anywhere = pl.BlockSpec(memory_space=pl.ANY)
    diag, fock = pl.pallas_call(
        functools.partial(exchange_kernel, aux_group ** (-0.5)),
        out_shape=(
            jax.ShapeDtypeStruct((rows, TILE), jnp.float32),
            jax.ShapeDtypeStruct((rows, W), bf16),
        ),
        in_specs=[pl.BlockSpec(memory_space=pltpu.SMEM), anywhere, anywhere],
        out_specs=(anywhere, anywhere),
        scratch_shapes=[
            pltpu.VMEM((groups, W, W), bf16),
            pltpu.VMEM((groups, W, W), bf16),
            pltpu.VMEM((aux_count, W, W), bf16),
            pltpu.VMEM((aux_count // groups, W, W), bf16),
            pltpu.VMEM((rows, W), jnp.float32),
            pltpu.VMEM((units, 2, 2, PART, TILE), bf16),
            pltpu.VMEM((units, 2, 2, PART, TILE), bf16),
            pltpu.VMEM((units, 2, PART, TILE), bf16),
            pltpu.VMEM((units, 2, PART, TILE), bf16),
            pltpu.VMEM((rows, TILE), jnp.float32),
            pltpu.VMEM((rows, W), bf16),
            dma((groups,)),
            dma((aux_count,)),
            dma((units,)),
            dma((units,)),
            dma((groups, W // PIECE)),
            dma((groups, W // PIECE)),
        ]
        + [dma((units, 2)) for _ in range(8)],
        compiler_params=pltpu.CompilerParams(collective_id=0, has_side_effects=True),
    )(listed, density, three_centre)
    wide = min(cols, 1024)
    result, diag = pl.pallas_call(
        apply_kernel,
        out_shape=(
            jax.ShapeDtypeStruct((rows, cols), bf16),
            jax.ShapeDtypeStruct((rows, TILE), jnp.float32),
        ),
        grid=(groups, cols // wide),
        in_specs=[
            pl.BlockSpec(memory_space=pltpu.SMEM),
            pl.BlockSpec((W, W), lambda g, n: (g, 0)),
            pl.BlockSpec((W, wide), lambda g, n: (g, n)),
            pl.BlockSpec((W, TILE), lambda g, n: (g, 0)),
        ],
        out_specs=(
            pl.BlockSpec((W, wide), lambda g, n: (g, n)),
            pl.BlockSpec((W, TILE), lambda g, n: (g, 0)),
        ),
        scratch_shapes=[pltpu.VMEM((W, wide), bf16)],
    )(listed, fock, density, diag)
    return diag, result


def takes_whole(mesh, density, listed, three_centre):
    row_count, col_count = mesh.shape["row"], mesh.shape["col"]
    rows = density.shape[0] // row_count
    cols = density.shape[1] // col_count
    aux_count = three_centre.shape[0] // (row_count * col_count)
    if rows % W or cols % rows or col_count != 4 or col_count * TILE != W:
        return False
    return aux_count % (rows // W) == 0


def solution(mesh):
    placed = (P("row", "col"), P("row", "col"), P(("row", "col"), None, None))

    def mapped(body):
        return jax.shard_map(
            body,
            mesh=mesh,
            in_specs=placed,
            out_specs=(P("row", "col"), P("row", "col")),
            check_vma=False,
        )

    def run(density, listed, three_centre):
        whole = takes_whole(mesh, density, listed, three_centre)
        return mapped(per_device_whole if whole else per_device)(density, listed, three_centre)

    return run
```

```python
import functools

import jax
import jax.numpy as jnp
from jax import lax
from jax.experimental import pallas as pl
from jax.experimental.pallas import tpu as pltpu
from jax.sharding import PartitionSpec as P

TILE = 128
W = 512
SUP = W // TILE
UNIT = W // 2
PART = UNIT // 2
PIECE = 32
BAND = 512
MESH = pl.DeviceIdType.MESH


def from_root(value, axis, root):
    mine = lax.axis_index(axis) == root
    return lax.psum(jnp.where(mine, value, jnp.zeros_like(value)), axis)


def partner_2(block, axis, stride):
    count = lax.axis_size(axis)
    route = []
    for low in range(count):
        high = low | 1 << stride
        if high != low and high < count:
            route += [(low, high), (high, low)]
    return lax.ppermute(block, axis, route)


def halve_rows(values, row_index, levels, sender):
    for bit_level in reversed(range(levels)):
        middle = values.shape[0] // 2
        lower_half = row_index // 2**bit_level % 2 == 0
        kept_rows = jnp.where(lower_half, values[:middle], values[middle:])
        sent_rows = jnp.where(lower_half, values[middle:], values[:middle])
        values = kept_rows + sender(sent_rows, bit_level)
    return values


def per_device(density, listed, three_centre):
    tile_rows = listed.shape[0]
    tile_cols = listed.shape[1]
    quad_tiles = max(tile_rows, 4)
    groups_dev = quad_tiles // 4
    aux_count = three_centre.shape[0]
    col_count = lax.axis_size("col")
    row_index = lax.axis_index("row")
    col_index = lax.axis_index("col")
    masked = (
        density.reshape(tile_rows, TILE, tile_cols, TILE)
        * listed[:, None, :, None].astype(jnp.bfloat16)
    ).reshape(tile_rows * TILE, tile_cols * TILE)
    quad_start = row_index * tile_rows // quad_tiles * quad_tiles
    col_offset = quad_start % tile_cols * TILE
    portion = lax.dynamic_slice_in_dim(masked, col_offset, quad_tiles * TILE, 1)
    diagonal = from_root(portion, "col", quad_start // tile_cols)
    joined = jnp.concatenate([diagonal, masked], axis=1)
    levels = (quad_tiles // tile_rows).bit_length() - 1
    for bit_level in range(levels):
        partner = partner_2(joined, "row", bit_level)
        lower_half = row_index // 2**bit_level % 2 == 0
        joined = jnp.where(
            lower_half,
            jnp.concatenate([joined, partner], axis=0),
            jnp.concatenate([partner, joined], axis=0),
        )
    quad_block = joined[:, : quad_tiles * TILE]
    quad_density = joined[:, quad_tiles * TILE :]
    group_ids = jnp.arange(groups_dev, dtype=jnp.int32)
    exchange_quad = jnp.zeros((groups_dev, W, W), jnp.float32)
    for aux_slot in range(aux_count):
        group_slot = (col_index * aux_count + aux_slot) % groups_dev
        density_sub = lax.dynamic_slice(quad_block, (group_slot * W, group_slot * W), (W, W))
        aux_block = three_centre[aux_slot]
        half_product = jnp.dot(aux_block, density_sub, preferred_element_type=jnp.float32).astype(
            jnp.bfloat16
        )
        contribution = lax.dot_general(
            half_product, aux_block, (((1,), (1,)), ((), ())), preferred_element_type=jnp.float32
        )
        exchange_quad = exchange_quad + jnp.where(
            (group_ids == group_slot)[:, None, None], contribution[None], 0.0
        )
    aux_group = aux_count * col_count * 4 // tile_rows
    exchange_quad = (exchange_quad * aux_group ** (-0.5)).reshape(quad_tiles * TILE, W)
    column_share = lax.psum_scatter(exchange_quad, "col", scatter_dimension=1, tiled=True)
    exchange_diag = halve_rows(
        column_share,
        row_index,
        levels,
        lambda sent_rows, bit_level: partner_2(sent_rows, "row", bit_level),
    )
    fock_rounded = lax.all_gather(exchange_diag.astype(jnp.bfloat16), "col", axis=1, tiled=True)
    rows_here = tile_rows * TILE
    segment_rows = min(rows_here, W)
    segment_count = rows_here // segment_rows
    within_quad = (row_index * tile_rows - quad_start) * TILE
    products = []
    for segment in range(segment_count):
        group_position = (within_quad + segment * segment_rows) // W
        dens_rows = lax.dynamic_slice_in_dim(quad_density, group_position * W, W, 0)
        fock_part = fock_rounded[segment * segment_rows : (segment + 1) * segment_rows]
        products.append(
            jnp.dot(fock_part, dens_rows, preferred_element_type=jnp.float32) * W ** (-0.5)
        )
    exchange_density = jnp.concatenate(products, axis=0).astype(jnp.bfloat16)
    return (exchange_diag, exchange_density)


def mask_tile(tile, flag):
    return tile * jnp.full(tile.shape, flag.astype(jnp.float32)).astype(jnp.bfloat16)


def exchange_kernel(
    scale, listed, density, three_centre, diag_out, fock_out,
    raw, block, coef, half, partial, send_1, recv_1, send_2, recv_2, diag, fock,
    raw_sem, coef_sem, diag_sem, fock_sem, bc_send, bc_recv, rs1_send, rs1_recv,
    rs2_send, rs2_recv, ag1_send, ag1_recv, ag2_send, ag2_recv,
):
    tile_rows, tile_cols = listed.shape
    groups = tile_rows // SUP
    units = groups * (W // UNIT)
    aux_count = three_centre.shape[0]
    row = lax.axis_index("row")
    me = lax.axis_index("col")
    x, y = me % 2, me // 2
    xn, yn = me + 1 - 2 * x, me + 2 - 4 * y
    far = xn + yn - me
    near = (xn, yn)
    first_tile = row * tile_rows
    owner = first_tile // tile_cols
    tile_off = first_tile % tile_cols
    ox, oy = owner % 2, owner // 2
    rx, ry = (x + ox) % 2, (y + oy) % 2
    even = (rx + ry + 1) % 2
    is_owner = rx + ry == 0
    hop_to = (xn * even + yn * (1 - even), yn * even + xn * (1 - even))
    last_of = (rx + 2 * (1 - ry) == 0, ry + 2 * (1 - rx) == 0)
    relays_of = (
        (rx + ry) * (rx + 1 - ry) > 0,
        (rx + ry) * (ry + 1 - rx) > 0,
    )

    def remote(src, dst, send_sem, recv_sem, target):
        return pltpu.make_async_remote_copy(
            src_ref=src, dst_ref=dst, send_sem=send_sem, recv_sem=recv_sem,
            device_id=(row, target), device_id_type=MESH,
        )

    def raw_copy(g):
        columns = pl.ds(pl.multiple_of((tile_off + g * SUP) * TILE, TILE), W)
        return pltpu.make_async_copy(
            density.at[pl.ds(g * W, W), columns], raw.at[g], raw_sem.at[g]
        )

    def coef_copy(q):
        return pltpu.make_async_copy(three_centre.at[q], coef.at[q], coef_sem.at[q])

    per_path = W // PIECE // 2

    def piece(g, i):
        part = block.at[g, pl.ds(i * PIECE, PIECE)]
        return remote(part, part, bc_send.at[g, i], bc_recv.at[g, i], hop_to[i // per_path])

    @pl.when(is_owner)
    def _():
        for g in range(groups):
            raw_copy(g).start()

    barrier = pltpu.get_barrier_semaphore()
    for neighbour in near:
        pl.semaphore_signal(barrier, inc=1, device_id=(row, neighbour), device_id_type=MESH)
    for q in range(aux_count):
        coef_copy(q).start()
    pl.semaphore_wait(barrier, 2)

    order = [s + h * per_path for s in range(per_path) for h in range(2)]

    @pl.when(is_owner)
    def _():
        for g in range(groups):
            raw_copy(g).wait()
            for i in order:
                rows = pl.ds(i * PIECE, PIECE)
                for j in range(SUP):
                    cols = pl.ds(j * TILE, TILE)
                    flag = listed[g * SUP + i * PIECE // TILE, tile_off + g * SUP + j]
                    block[g, rows, cols] = mask_tile(raw[g, rows, cols], flag)
                piece(g, i).start()

    def relay(g, pieces):
        for i in pieces:
            @pl.when(relays_of[i // per_path])
            def _():
                piece(g, i).wait_recv()
                piece(g, i).start()

    def stage_1(u, h):
        return remote(send_1.at[u, h], recv_1.at[u, h], rs1_send.at[u, h], rs1_recv.at[u, h], near[h])

    def stage_2(u, h):
        return remote(
            send_2.at[u, h], recv_2.at[u, h], rs2_send.at[u, h], rs2_recv.at[u, h], near[1 - h]
        )

    def columns_of(dev):
        return pl.ds(pl.multiple_of(dev * TILE, TILE), TILE)

    def rows_of(u, h):
        return pl.ds(u * UNIT + h * PART, PART)

    def gather_1(u, axis):
        part = fock.at[pl.ds(u * UNIT, UNIT), columns_of(me)]
        return remote(part, part, ag1_send.at[u, axis], ag1_recv.at[u, axis], near[axis])

    def gather_2(u, axis):
        part = fock.at[rows_of(u, axis), columns_of(near[1 - axis])]
        return remote(part, part, ag2_send.at[u, axis], ag2_recv.at[u, axis], near[axis])

    def diag_copy(u):
        rows = pl.ds(u * UNIT, UNIT)
        return pltpu.make_async_copy(diag.at[rows], diag_out.at[rows], diag_sem.at[u])

    def fock_copy(u):
        rows = pl.ds(u * UNIT, UNIT)
        return pltpu.make_async_copy(fock.at[rows], fock_out.at[rows], fock_sem.at[u])

    for g in range(groups):
        relay(g, order)
    for q in range(aux_count):
        coef_copy(q).wait()
    for g in range(groups):
        members = list(range(g, aux_count, groups))
        for h in range(2):
            @pl.when(last_of[h])
            def _():
                for s in range(per_path):
                    piece(g, s + h * per_path).wait_recv()
        for n, q in enumerate(members):
            half[n] = jnp.dot(coef[q], block[g], preferred_element_type=jnp.float32).astype(jnp.bfloat16)
        for v in range(W // UNIT):
            u = g * (W // UNIT) + v
            rows = pl.ds(v * UNIT, UNIT)
            for n, q in enumerate(members):
                term = lax.dot_general(
                    half[n, rows], coef[q], (((1,), (1,)), ((), ())),
                    preferred_element_type=jnp.float32,
                )
                if n == 0:
                    partial[pl.ds(u * UNIT, UNIT)] = term
                else:
                    partial[pl.ds(u * UNIT, UNIT)] += term
            for h in range(2):
                send_1[u, h, 0] = partial[rows_of(u, h), columns_of(near[h])].astype(jnp.bfloat16)
                send_1[u, h, 1] = partial[rows_of(u, h), columns_of(far)].astype(jnp.bfloat16)
                stage_1(u, h).start()

    for phase, step in [(p, u) for p in range(4) for u in range(units)]:
        if phase == 0:
            u = step
            for h in range(2):
                stage_1(u, h).wait_recv()
                send_2[u, h] = (
                    partial[rows_of(u, h), columns_of(near[1 - h])]
                    + recv_1[u, h, 1].astype(jnp.float32)
                ).astype(jnp.bfloat16)
                stage_2(u, h).start()
        if phase == 1:
            u = step
            for h in range(2):
                stage_2(u, h).wait_recv()
                total = (
                    partial[rows_of(u, h), columns_of(me)]
                    + recv_1[u, h, 0].astype(jnp.float32)
                    + recv_2[u, h].astype(jnp.float32)
                ) * scale
                diag[rows_of(u, h)] = total
                fock[rows_of(u, h), columns_of(me)] = total.astype(jnp.bfloat16)
            for axis in range(2):
                gather_1(u, axis).start()
            diag_copy(u).start()
        if phase == 2:
            u = step
            for axis in range(2):
                gather_1(u, 1 - axis).wait_recv()
                gather_2(u, axis).start()
        if phase == 3:
            u = step
            for axis in range(2):
                gather_2(u, axis).wait_recv()
            fock_copy(u).start()
    for g in range(groups):
        for i in order:
            @pl.when(jnp.logical_not(last_of[i // per_path]))
            def _():
                piece(g, i).wait_send()
    for u in range(units):
        for h in range(2):
            stage_1(u, h).wait_send()
            stage_2(u, h).wait_send()
            gather_1(u, h).wait_send()
            gather_2(u, h).wait_send()
        diag_copy(u).wait()
        fock_copy(u).wait()


def apply_kernel(
    listed, fock_in, density, diag_in, result, diag_out, fock, dens, out, diag,
    fock_sem, dens_sem, out_sem, diag_sem,
):
    rows, cols = density.shape
    groups = rows // W

    def fock_copy(g):
        part = pl.ds(g * W, W)
        return pltpu.make_async_copy(fock_in.at[part], fock.at[part], fock_sem.at[g])

    def dens_copy(t):
        part = pl.ds(t * TILE, TILE)
        return pltpu.make_async_copy(density.at[part], dens.at[part], dens_sem.at[t])

    def out_copy(m):
        part = pl.ds(m * BAND, BAND)
        return pltpu.make_async_copy(out.at[part], result.at[part], out_sem.at[m])

    for g in range(groups):
        for t in range(g * SUP, (g + 1) * SUP):
            dens_copy(t).start()
        fock_copy(g).start()
    pltpu.make_async_copy(diag_in, diag, diag_sem.at[0]).start()
    for g in range(groups):
        for t in range(g * SUP, (g + 1) * SUP):
            dens_copy(t).wait()
            part = pl.ds(t * TILE, TILE)
            for j in range(cols // TILE):
                span = pl.ds(j * TILE, TILE)
                dens[part, span] = mask_tile(dens[part, span], listed[t, j])
        fock_copy(g).wait()
        if g == 0:
            pltpu.make_async_copy(diag_in, diag, diag_sem.at[0]).wait()
            pltpu.make_async_copy(diag, diag_out, diag_sem.at[1]).start()
        for m in range(g * W // BAND, (g + 1) * W // BAND):
            part = pl.ds(m * BAND, BAND)
            product = jnp.dot(
                fock[part], dens[pl.ds(g * W, W)], preferred_element_type=jnp.float32
            )
            out[part] = (product * W ** (-0.5)).astype(jnp.bfloat16)
            out_copy(m).start()
    for m in range(rows // BAND):
        out_copy(m).wait()
    pltpu.make_async_copy(diag, diag_out, diag_sem.at[1]).wait()


def per_device_whole(density, listed, three_centre):
    rows, cols = density.shape
    groups = rows // W
    units = rows // UNIT
    aux_count = three_centre.shape[0]
    aux_group = aux_count * lax.axis_size("col") // groups
    bf16, dma = jnp.bfloat16, pltpu.SemaphoreType.DMA
    anywhere = pl.BlockSpec(memory_space=pl.ANY)
    diag, fock = pl.pallas_call(
        functools.partial(exchange_kernel, aux_group ** (-0.5)),
        out_shape=(
            jax.ShapeDtypeStruct((rows, TILE), jnp.float32),
            jax.ShapeDtypeStruct((rows, W), bf16),
        ),
        in_specs=[pl.BlockSpec(memory_space=pltpu.SMEM), anywhere, anywhere],
        out_specs=(anywhere, anywhere),
        scratch_shapes=[
            pltpu.VMEM((groups, W, W), bf16),
            pltpu.VMEM((groups, W, W), bf16),
            pltpu.VMEM((aux_count, W, W), bf16),
            pltpu.VMEM((aux_count // groups, W, W), bf16),
            pltpu.VMEM((rows, W), jnp.float32),
            pltpu.VMEM((units, 2, 2, PART, TILE), bf16),
            pltpu.VMEM((units, 2, 2, PART, TILE), bf16),
            pltpu.VMEM((units, 2, PART, TILE), bf16),
            pltpu.VMEM((units, 2, PART, TILE), bf16),
            pltpu.VMEM((rows, TILE), jnp.float32),
            pltpu.VMEM((rows, W), bf16),
            dma((groups,)),
            dma((aux_count,)),
            dma((units,)),
            dma((units,)),
            dma((groups, W // PIECE)),
            dma((groups, W // PIECE)),
        ]
        + [dma((units, 2)) for _ in range(8)],
        compiler_params=pltpu.CompilerParams(collective_id=0, has_side_effects=True),
    )(listed, density, three_centre)
    result, diag = pl.pallas_call(
        apply_kernel,
        out_shape=(
            jax.ShapeDtypeStruct((rows, cols), bf16),
            jax.ShapeDtypeStruct((rows, TILE), jnp.float32),
        ),
        in_specs=[pl.BlockSpec(memory_space=pltpu.SMEM), anywhere, anywhere, anywhere],
        out_specs=(anywhere, anywhere),
        scratch_shapes=[
            pltpu.VMEM((rows, W), bf16),
            pltpu.VMEM((rows, cols), bf16),
            pltpu.VMEM((rows, cols), bf16),
            pltpu.VMEM((rows, TILE), jnp.float32),
            dma((groups,)),
            dma((rows // TILE,)),
            dma((rows // BAND,)),
            dma((2,)),
        ],
    )(listed, fock, density, diag)
    return diag, result


def takes_whole(mesh, density, listed, three_centre):
    row_count, col_count = mesh.shape["row"], mesh.shape["col"]
    rows = density.shape[0] // row_count
    cols = density.shape[1] // col_count
    aux_count = three_centre.shape[0] // (row_count * col_count)
    if rows % W or cols % rows or col_count != 4 or col_count * TILE != W:
        return False
    return aux_count % (rows // W) == 0


def solution(mesh):
    placed = (P("row", "col"), P("row", "col"), P(("row", "col"), None, None))

    def mapped(body):
        return jax.shard_map(
            body,
            mesh=mesh,
            in_specs=placed,
            out_specs=(P("row", "col"), P("row", "col")),
            check_vma=False,
        )

    def run(density, listed, three_centre):
        whole = takes_whole(mesh, density, listed, three_centre)
        return mapped(per_device_whole if whole else per_device)(density, listed, three_centre)

    return run
```

```python
import functools

import jax
import jax.numpy as jnp
from jax import lax
from jax.experimental import pallas as pl
from jax.experimental.pallas import tpu as pltpu
from jax.sharding import PartitionSpec as P

TILE = 128
W = 512
SUP = W // TILE
UNIT = W // 2
PART = UNIT // 2
PIECE = 32
BAND = 256
MESH = pl.DeviceIdType.MESH


def from_root(value, axis, root):
    mine = lax.axis_index(axis) == root
    return lax.psum(jnp.where(mine, value, jnp.zeros_like(value)), axis)


def partner_2(block, axis, stride):
    count = lax.axis_size(axis)
    route = []
    for low in range(count):
        high = low | 1 << stride
        if high != low and high < count:
            route += [(low, high), (high, low)]
    return lax.ppermute(block, axis, route)


def halve_rows(values, row_index, levels, sender):
    for bit_level in reversed(range(levels)):
        middle = values.shape[0] // 2
        lower_half = row_index // 2**bit_level % 2 == 0
        kept_rows = jnp.where(lower_half, values[:middle], values[middle:])
        sent_rows = jnp.where(lower_half, values[middle:], values[:middle])
        values = kept_rows + sender(sent_rows, bit_level)
    return values


def per_device(density, listed, three_centre):
    tile_rows = listed.shape[0]
    tile_cols = listed.shape[1]
    quad_tiles = max(tile_rows, 4)
    groups_dev = quad_tiles // 4
    aux_count = three_centre.shape[0]
    col_count = lax.axis_size("col")
    row_index = lax.axis_index("row")
    col_index = lax.axis_index("col")
    masked = (
        density.reshape(tile_rows, TILE, tile_cols, TILE)
        * listed[:, None, :, None].astype(jnp.bfloat16)
    ).reshape(tile_rows * TILE, tile_cols * TILE)
    quad_start = row_index * tile_rows // quad_tiles * quad_tiles
    col_offset = quad_start % tile_cols * TILE
    portion = lax.dynamic_slice_in_dim(masked, col_offset, quad_tiles * TILE, 1)
    diagonal = from_root(portion, "col", quad_start // tile_cols)
    joined = jnp.concatenate([diagonal, masked], axis=1)
    levels = (quad_tiles // tile_rows).bit_length() - 1
    for bit_level in range(levels):
        partner = partner_2(joined, "row", bit_level)
        lower_half = row_index // 2**bit_level % 2 == 0
        joined = jnp.where(
            lower_half,
            jnp.concatenate([joined, partner], axis=0),
            jnp.concatenate([partner, joined], axis=0),
        )
    quad_block = joined[:, : quad_tiles * TILE]
    quad_density = joined[:, quad_tiles * TILE :]
    group_ids = jnp.arange(groups_dev, dtype=jnp.int32)
    exchange_quad = jnp.zeros((groups_dev, W, W), jnp.float32)
    for aux_slot in range(aux_count):
        group_slot = (col_index * aux_count + aux_slot) % groups_dev
        density_sub = lax.dynamic_slice(quad_block, (group_slot * W, group_slot * W), (W, W))
        aux_block = three_centre[aux_slot]
        half_product = jnp.dot(aux_block, density_sub, preferred_element_type=jnp.float32).astype(
            jnp.bfloat16
        )
        contribution = lax.dot_general(
            half_product, aux_block, (((1,), (1,)), ((), ())), preferred_element_type=jnp.float32
        )
        exchange_quad = exchange_quad + jnp.where(
            (group_ids == group_slot)[:, None, None], contribution[None], 0.0
        )
    aux_group = aux_count * col_count * 4 // tile_rows
    exchange_quad = (exchange_quad * aux_group ** (-0.5)).reshape(quad_tiles * TILE, W)
    column_share = lax.psum_scatter(exchange_quad, "col", scatter_dimension=1, tiled=True)
    exchange_diag = halve_rows(
        column_share,
        row_index,
        levels,
        lambda sent_rows, bit_level: partner_2(sent_rows, "row", bit_level),
    )
    fock_rounded = lax.all_gather(exchange_diag.astype(jnp.bfloat16), "col", axis=1, tiled=True)
    rows_here = tile_rows * TILE
    segment_rows = min(rows_here, W)
    segment_count = rows_here // segment_rows
    within_quad = (row_index * tile_rows - quad_start) * TILE
    products = []
    for segment in range(segment_count):
        group_position = (within_quad + segment * segment_rows) // W
        dens_rows = lax.dynamic_slice_in_dim(quad_density, group_position * W, W, 0)
        fock_part = fock_rounded[segment * segment_rows : (segment + 1) * segment_rows]
        products.append(
            jnp.dot(fock_part, dens_rows, preferred_element_type=jnp.float32) * W ** (-0.5)
        )
    exchange_density = jnp.concatenate(products, axis=0).astype(jnp.bfloat16)
    return (exchange_diag, exchange_density)


def mask_tile(tile, flag):
    return tile * jnp.full(tile.shape, flag.astype(jnp.float32)).astype(jnp.bfloat16)


def exchange_kernel(
    scale, listed, density, three_centre, diag_out, fock_out, masked_out,
    dens, dens_sem, masked_sem,
    raw, block, coef, half, partial, send_1, recv_1, send_2, recv_2, diag, fock,
    raw_sem, coef_sem, diag_sem, fock_sem, bc_send, bc_recv, rs1_send, rs1_recv,
    rs2_send, rs2_recv, ag1_send, ag1_recv, ag2_send, ag2_recv,
):
    tile_rows, tile_cols = listed.shape
    groups = tile_rows // SUP
    units = groups * (W // UNIT)
    aux_count = three_centre.shape[0]
    row = lax.axis_index("row")
    me = lax.axis_index("col")
    x, y = me % 2, me // 2
    xn, yn = me + 1 - 2 * x, me + 2 - 4 * y
    far = xn + yn - me
    near = (xn, yn)
    first_tile = row * tile_rows
    owner = first_tile // tile_cols
    tile_off = first_tile % tile_cols
    ox, oy = owner % 2, owner // 2
    rx, ry = (x + ox) % 2, (y + oy) % 2
    even = (rx + ry + 1) % 2
    is_owner = rx + ry == 0
    hop_to = (xn * even + yn * (1 - even), yn * even + xn * (1 - even))
    last_of = (rx + 2 * (1 - ry) == 0, ry + 2 * (1 - rx) == 0)
    relays_of = (
        (rx + ry) * (rx + 1 - ry) > 0,
        (rx + ry) * (ry + 1 - rx) > 0,
    )

    def remote(src, dst, send_sem, recv_sem, target):
        return pltpu.make_async_remote_copy(
            src_ref=src, dst_ref=dst, send_sem=send_sem, recv_sem=recv_sem,
            device_id=(row, target), device_id_type=MESH,
        )

    def raw_copy(g):
        columns = pl.ds(pl.multiple_of((tile_off + g * SUP) * TILE, TILE), W)
        return pltpu.make_async_copy(
            density.at[pl.ds(g * W, W), columns], raw.at[g], raw_sem.at[g]
        )

    def coef_copy(q):
        return pltpu.make_async_copy(three_centre.at[q], coef.at[q], coef_sem.at[q])

    per_path = W // PIECE // 2

    def piece(g, i):
        part = block.at[g, pl.ds(i * PIECE, PIECE)]
        return remote(part, part, bc_send.at[g, i], bc_recv.at[g, i], hop_to[i // per_path])

    @pl.when(is_owner)
    def _():
        for g in range(groups):
            raw_copy(g).start()

    def dens_copy(t):
        part = pl.ds(t * TILE, TILE)
        return pltpu.make_async_copy(density.at[part], dens.at[part], dens_sem.at[t])

    def masked_copy(t):
        part = pl.ds(t * TILE, TILE)
        return pltpu.make_async_copy(dens.at[part], masked_out.at[part], masked_sem.at[t])

    barrier = pltpu.get_barrier_semaphore()
    for neighbour in near:
        pl.semaphore_signal(barrier, inc=1, device_id=(row, neighbour), device_id_type=MESH)
    for q in range(aux_count):
        coef_copy(q).start()
    for t in range(tile_rows):
        dens_copy(t).start()
    pl.semaphore_wait(barrier, 2)

    order = [s + h * per_path for s in range(per_path) for h in range(2)]

    @pl.when(is_owner)
    def _():
        for g in range(groups):
            raw_copy(g).wait()
            for i in order:
                rows = pl.ds(i * PIECE, PIECE)
                for j in range(SUP):
                    cols = pl.ds(j * TILE, TILE)
                    flag = listed[g * SUP + i * PIECE // TILE, tile_off + g * SUP + j]
                    block[g, rows, cols] = mask_tile(raw[g, rows, cols], flag)
                piece(g, i).start()

    def relay(g, pieces):
        for i in pieces:
            @pl.when(relays_of[i // per_path])
            def _():
                piece(g, i).wait_recv()
                piece(g, i).start()

    def stage_1(u, h):
        return remote(send_1.at[u, h], recv_1.at[u, h], rs1_send.at[u, h], rs1_recv.at[u, h], near[h])

    def stage_2(u, h):
        return remote(
            send_2.at[u, h], recv_2.at[u, h], rs2_send.at[u, h], rs2_recv.at[u, h], near[1 - h]
        )

    def columns_of(dev):
        return pl.ds(pl.multiple_of(dev * TILE, TILE), TILE)

    def rows_of(u, h):
        return pl.ds(u * UNIT + h * PART, PART)

    def gather_1(u, axis):
        part = fock.at[pl.ds(u * UNIT, UNIT), columns_of(me)]
        return remote(part, part, ag1_send.at[u, axis], ag1_recv.at[u, axis], near[axis])

    def gather_2(u, axis):
        part = fock.at[rows_of(u, axis), columns_of(near[1 - axis])]
        return remote(part, part, ag2_send.at[u, axis], ag2_recv.at[u, axis], near[axis])

    def diag_copy(u):
        rows = pl.ds(u * UNIT, UNIT)
        return pltpu.make_async_copy(diag.at[rows], diag_out.at[rows], diag_sem.at[u])

    def fock_copy(u):
        rows = pl.ds(u * UNIT, UNIT)
        return pltpu.make_async_copy(fock.at[rows], fock_out.at[rows], fock_sem.at[u])

    for g in range(groups):
        relay(g, order)
    for t in range(tile_rows):
        dens_copy(t).wait()
        part = pl.ds(t * TILE, TILE)
        for j in range(tile_cols):
            span = pl.ds(j * TILE, TILE)
            dens[part, span] = mask_tile(dens[part, span], listed[t, j])
        masked_copy(t).start()
    for q in range(aux_count):
        coef_copy(q).wait()
    for g in range(groups):
        members = list(range(g, aux_count, groups))
        for h in range(2):
            @pl.when(last_of[h])
            def _():
                for s in range(per_path):
                    piece(g, s + h * per_path).wait_recv()
        for n, q in enumerate(members):
            half[n] = jnp.dot(coef[q], block[g], preferred_element_type=jnp.float32).astype(jnp.bfloat16)
        for v in range(W // UNIT):
            u = g * (W // UNIT) + v
            rows = pl.ds(v * UNIT, UNIT)
            for n, q in enumerate(members):
                term = lax.dot_general(
                    half[n, rows], coef[q], (((1,), (1,)), ((), ())),
                    preferred_element_type=jnp.float32,
                )
                if n == 0:
                    partial[pl.ds(u * UNIT, UNIT)] = term
                else:
                    partial[pl.ds(u * UNIT, UNIT)] += term
            for h in range(2):
                send_1[u, h, 0] = partial[rows_of(u, h), columns_of(near[h])].astype(jnp.bfloat16)
                send_1[u, h, 1] = partial[rows_of(u, h), columns_of(far)].astype(jnp.bfloat16)
                stage_1(u, h).start()

    for phase, step in [(p, u) for p in range(4) for u in range(units)]:
        if phase == 0:
            u = step
            for h in range(2):
                stage_1(u, h).wait_recv()
                send_2[u, h] = (
                    partial[rows_of(u, h), columns_of(near[1 - h])]
                    + recv_1[u, h, 1].astype(jnp.float32)
                ).astype(jnp.bfloat16)
                stage_2(u, h).start()
        if phase == 1:
            u = step
            for h in range(2):
                stage_2(u, h).wait_recv()
                total = (
                    partial[rows_of(u, h), columns_of(me)]
                    + recv_1[u, h, 0].astype(jnp.float32)
                    + recv_2[u, h].astype(jnp.float32)
                ) * scale
                diag[rows_of(u, h)] = total
                fock[rows_of(u, h), columns_of(me)] = total.astype(jnp.bfloat16)
            for axis in range(2):
                gather_1(u, axis).start()
            diag_copy(u).start()
        if phase == 2:
            u = step
            for axis in range(2):
                gather_1(u, 1 - axis).wait_recv()
                gather_2(u, axis).start()
        if phase == 3:
            u = step
            for axis in range(2):
                gather_2(u, axis).wait_recv()
            fock_copy(u).start()
    for g in range(groups):
        for i in order:
            @pl.when(jnp.logical_not(last_of[i // per_path]))
            def _():
                piece(g, i).wait_send()
    for u in range(units):
        for h in range(2):
            stage_1(u, h).wait_send()
            stage_2(u, h).wait_send()
            gather_1(u, h).wait_send()
            gather_2(u, h).wait_send()
        diag_copy(u).wait()
        fock_copy(u).wait()
    for t in range(tile_rows):
        masked_copy(t).wait()


def apply_kernel(fock, masked, diag, result, diag_out, out, out_sem, diag_sem):
    rows = masked.shape[0]

    def out_copy(m):
        part = pl.ds(m * BAND, BAND)
        return pltpu.make_async_copy(out.at[part], result.at[part], out_sem.at[m])

    pltpu.make_async_copy(diag, diag_out, diag_sem.at[0]).start()
    for m in range(rows // BAND):
        part = pl.ds(m * BAND, BAND)
        support = pl.ds(m * BAND // W * W, W)
        product = jnp.dot(fock[part], masked[support], preferred_element_type=jnp.float32)
        out[part] = (product * W ** (-0.5)).astype(jnp.bfloat16)
        out_copy(m).start()
    for m in range(rows // BAND):
        out_copy(m).wait()
    pltpu.make_async_copy(diag, diag_out, diag_sem.at[0]).wait()


def per_device_whole(density, listed, three_centre):
    rows, cols = density.shape
    groups = rows // W
    units = rows // UNIT
    aux_count = three_centre.shape[0]
    aux_group = aux_count * lax.axis_size("col") // groups
    bf16, dma = jnp.bfloat16, pltpu.SemaphoreType.DMA
    inside = pl.BlockSpec(memory_space=pltpu.VMEM)
    anywhere = pl.BlockSpec(memory_space=pl.ANY)
    diag, fock, masked = pl.pallas_call(
        functools.partial(exchange_kernel, aux_group ** (-0.5)),
        out_shape=(
            jax.ShapeDtypeStruct((rows, TILE), jnp.float32),
            jax.ShapeDtypeStruct((rows, W), bf16),
            jax.ShapeDtypeStruct((rows, cols), bf16),
        ),
        in_specs=[pl.BlockSpec(memory_space=pltpu.SMEM), anywhere, anywhere],
        out_specs=(anywhere, anywhere, anywhere),
        scratch_shapes=[
            pltpu.VMEM((rows, cols), bf16),
            dma((rows // TILE,)),
            dma((rows // TILE,)),
            pltpu.VMEM((groups, W, W), bf16),
            pltpu.VMEM((groups, W, W), bf16),
            pltpu.VMEM((aux_count, W, W), bf16),
            pltpu.VMEM((aux_count // groups, W, W), bf16),
            pltpu.VMEM((rows, W), jnp.float32),
            pltpu.VMEM((units, 2, 2, PART, TILE), bf16),
            pltpu.VMEM((units, 2, 2, PART, TILE), bf16),
            pltpu.VMEM((units, 2, PART, TILE), bf16),
            pltpu.VMEM((units, 2, PART, TILE), bf16),
            pltpu.VMEM((rows, TILE), jnp.float32),
            pltpu.VMEM((rows, W), bf16),
            dma((groups,)),
            dma((aux_count,)),
            dma((units,)),
            dma((units,)),
            dma((groups, W // PIECE)),
            dma((groups, W // PIECE)),
        ]
        + [dma((units, 2)) for _ in range(8)],
        compiler_params=pltpu.CompilerParams(
            collective_id=0, has_side_effects=True, vmem_limit_bytes=24 * 2**20
        ),
    )(listed, density, three_centre)
    result, diag = pl.pallas_call(
        apply_kernel,
        out_shape=(
            jax.ShapeDtypeStruct((rows, cols), bf16),
            jax.ShapeDtypeStruct((rows, TILE), jnp.float32),
        ),
        in_specs=[inside, inside, inside],
        out_specs=(anywhere, anywhere),
        scratch_shapes=[
            pltpu.VMEM((rows, cols), bf16),
            dma((rows // BAND,)),
            dma((1,)),
        ],
        compiler_params=pltpu.CompilerParams(vmem_limit_bytes=20 * 2**20),
    )(fock, masked, diag)
    return diag, result


def takes_whole(mesh, density, listed, three_centre):
    row_count, col_count = mesh.shape["row"], mesh.shape["col"]
    rows = density.shape[0] // row_count
    cols = density.shape[1] // col_count
    aux_count = three_centre.shape[0] // (row_count * col_count)
    if rows % W or cols % rows or col_count != 4 or col_count * TILE != W:
        return False
    return aux_count % (rows // W) == 0


def solution(mesh):
    placed = (P("row", "col"), P("row", "col"), P(("row", "col"), None, None))

    def mapped(body):
        return jax.shard_map(
            body,
            mesh=mesh,
            in_specs=placed,
            out_specs=(P("row", "col"), P("row", "col")),
            check_vma=False,
        )

    def run(density, listed, three_centre):
        whole = takes_whole(mesh, density, listed, three_centre)
        return mapped(per_device_whole if whole else per_device)(density, listed, three_centre)

    return run
```
